32 devices in a mesh: head: 8 (over y, x, core), tail: 4 (over z).
Axes of the slice: x: 2, y: 2, z: 4, core: 2. Of those that a mesh axis runs over, the one named last changes fastest.
Arguments:
- head_emb: float32 [8, 512, 256], P('head'), may hold values from -1.5 to 1.5
- tail_emb: float32 [4, 2048, 256], P('tail'), may hold values from -1.5 to 1.5
- relations: float32 [4096, 256], P(('head', 'tail')), may hold values from -0.375 to 0.375
- head_index: int32 [8, 4, 2, 1, 512], P('head', 'tail'), may hold values from 0 to 511
- tail_index: int32 [8, 4, 2, 1, 512], P('head', 'tail'), may hold values from 0 to 2047
- rel_index: int32 [8, 4, 2, 1, 512], P('head', 'tail'), may hold values from 0 to 15
- neg_index: int32 [8, 4, 2, 1, 512], P('head', 'tail'), may hold values from 0 to 2047
Outputs:
- head_grad: float32 [8, 512, 256], P('head', 'tail')
- tail_grad: float32 [4, 2048, 256], P('tail', 'head')
- rel_grad: float32 [4096, 256], P(('head', 'tail'))
The draws below stay inside these ranges and needn't reach their ends.
All inputs are finite; a program needn't handle non-finite values.
Results may differ from the reference program's by a relative error of at most 0.00028.
Values sent between devices are 32-bit elements; how exact they have to be, the bound alone decides.
A program may use at most 128 MiB of HBM per device.

```python
import math
import jax
import jax.numpy as jnp
import numpy as np
from jax import lax

D = 256
NREL = 16
B = 512
NEG = 512
STEPS = 2
BLOCKS = 1
EH = 512
ET = 2048
N_HEAD = 8
N_TAIL = 4


def place_ends(values, key, least, top_value):
    index_at = [jax.random.randint(jax.random.fold_in(key, axis), (), 0, length) for axis, length in enumerate(values.shape)]
    widest = values.shape.index(max(values.shape))
    beside = index_at[:widest] + [(index_at[widest] + 1) % values.shape[widest]] + index_at[widest + 1:]
    return values.at[tuple(index_at)].set(least).at[tuple(beside)].set(top_value)


def levels(key, extent, shards, low, high):
    def one(dim, shards_of):
        steps = jax.random.uniform(jax.random.fold_in(jax.random.fold_in(key, 6), dim), (shards_of,), jnp.float32, low / len(shards), high / len(shards))
        return jnp.repeat(jnp.exp(steps), extent[dim] // shards_of).reshape((-1,) + (1,) * (len(extent) - dim - 1))

    loudness = one(*shards[0])
    for cut in shards[1:]:
        loudness = loudness * one(*cut)
    return loudness


def cumulative_ranks(amount, slope):
    weights = [(1 << 20) // math.isqrt(rank ** slope) + 1 for rank in range(1, amount + 1)]
    width = 1 + sum(weights) // (1 << 30)
    return np.cumsum(np.array([max(1, weight // width) for weight in weights]))


def skewed_ids(rng, extent, count, lean):
    listing = cumulative_ranks(count, lean)
    ticket = jax.random.randint(jax.random.fold_in(rng, 1), extent, 0, int(listing[count - 1]))
    grade = jnp.searchsorted(jnp.asarray(listing, jnp.int32), ticket, side="right")
    return jax.random.permutation(jax.random.fold_in(rng, 2), count)[grade].astype(jnp.int32)


def scatter_about(rng, dims, scale, limit, cuts=(), held_as=jnp.bfloat16):
    level = levels(rng, dims, cuts, -0.22, 0.18) if cuts else 1.0
    entries = jax.random.normal(rng, dims, jnp.float32) * scale * level
    return jnp.minimum(jnp.maximum(entries, -limit), limit).astype(held_as)


def setup_inputs(seed: int = 0) -> dict:
    streams_of = jax.random.split(jax.random.key(seed), 8)
    return {
        "head_emb": scatter_about(streams_of[0], (N_HEAD, EH, D), 0.25, 1.5, ((0, 8),), jnp.float32),
        "tail_emb": scatter_about(streams_of[1], (N_TAIL, ET, D), 0.25, 1.5, ((0, 4),), jnp.float32),
        "relations": scatter_about(streams_of[2], (NREL * D, D), D ** -0.5, 0.375, ((0, 32),), jnp.float32),
        "head_index": place_ends(jax.random.randint(streams_of[3], (N_HEAD, N_TAIL, STEPS, BLOCKS, B), 0, EH), jax.random.fold_in(streams_of[3], 1), 0, EH - 1).astype(jnp.int32),
        "tail_index": place_ends(jax.random.randint(streams_of[4], (N_HEAD, N_TAIL, STEPS, BLOCKS, B), 0, ET), jax.random.fold_in(streams_of[4], 1), 0, ET - 1).astype(jnp.int32),
        "rel_index": place_ends(skewed_ids(streams_of[5], (N_HEAD, N_TAIL, STEPS, BLOCKS, B), NREL, 2), jax.random.fold_in(streams_of[5], 3), 0, NREL - 1).astype(jnp.int32),
        "neg_index": place_ends(jax.random.randint(streams_of[6], (N_HEAD, N_TAIL, STEPS, BLOCKS, NEG), 0, ET), jax.random.fold_in(streams_of[6], 1), 0, ET - 1).astype(jnp.int32),
    }


def reference(head_emb, tail_emb, relations, head_index, tail_index, rel_index, neg_index):
    highest = lax.Precision.HIGHEST
    rel_mats = relations.reshape(NREL, D, D)
    head_part = jnp.broadcast_to(jnp.arange(N_HEAD, dtype=jnp.int32)[:, None, None, None], (N_HEAD, N_TAIL, STEPS, BLOCKS))
    group = jnp.arange(N_TAIL, dtype=jnp.int32)[None, :, None, None]
    stepno = jnp.arange(STEPS, dtype=jnp.int32)[None, None, :, None]
    tail_part = jnp.broadcast_to((group - stepno) % N_TAIL, (N_HEAD, N_TAIL, STEPS, BLOCKS)).astype(jnp.int32)
    inputs = (head_part.reshape(-1), tail_part.reshape(-1), head_index.reshape(-1, B), tail_index.reshape(-1, B), rel_index.reshape(-1, B), neg_index.reshape(-1, NEG))

    def one_block(carry, items):
        grad_head, grad_tail, grad_rel = carry
        part_h, part_t, rows_h, rows_t, rows_r, rows_n = items
        head_vec = head_emb[part_h][rows_h]
        tail_vec = tail_emb[part_t][rows_t]
        negatives = tail_emb[part_t][rows_n]
        chosen = rel_mats[rows_r]
        query = jnp.einsum("bd,bde->be", head_vec, chosen, precision=highest)
        positive = jnp.sum(query * tail_vec, axis=1)
        negative = jnp.dot(query, negatives.T, precision=highest)
        coef = -jax.nn.sigmoid(-positive)
        weights = jax.nn.sigmoid(negative) / NEG
        factor = coef[:, None] * tail_vec + jnp.dot(weights, negatives, precision=highest)
        back = jnp.einsum("bde,be->bd", chosen, factor, precision=highest)
        grad_head = grad_head.at[part_h, rows_h].add(back)
        grad_tail = grad_tail.at[part_t, rows_t].add(coef[:, None] * query)
        grad_tail = grad_tail.at[part_t, rows_n].add(jnp.dot(weights.T, query, precision=highest))
        outer = jnp.einsum("bd,be->bde", head_vec, factor)
        grad_rel = grad_rel.at[rows_r].add(outer)
        return (grad_head, grad_tail, grad_rel), None

    start = (jnp.zeros((N_HEAD, EH, D), jnp.float32), jnp.zeros((N_TAIL, ET, D), jnp.float32), jnp.zeros((NREL, D, D), jnp.float32))
    (grad_head, grad_tail, grad_rel), unused = lax.scan(one_block, start, inputs)
    return grad_head, grad_tail, grad_rel.reshape(NREL * D, D)
```

```python
import functools
import jax
import jax.numpy as jnp
from jax import lax
from jax.experimental import pallas as pl
from jax.experimental.pallas import tpu as pltpu
from jax.sharding import PartitionSpec as P

F32 = jnp.float32
BF16 = jnp.bfloat16
VMEM_LIMIT = 60 * 1024 * 1024
NN = (((1,), (0,)), ((), ()))
NT = (((1,), (1,)), ((), ()))
TN = (((0,), (0,)), ((), ()))


def split(x):
    high = x.astype(BF16)
    return high, (x - high.astype(F32)).astype(BF16)


def dot(a, b, dims):
    return lax.dot_general(a, b, dims, preferred_element_type=F32)


def dot3(a, b, dims):
    return dot(a[0], b[0], dims) + (dot(a[0], b[1], dims) + dot(a[1], b[0], dims))


def log2(n):
    assert n & (n - 1) == 0
    return n.bit_length() - 1


class Bits:
    def __init__(self, sizes):
        self.names = [(axis, bit) for axis, size in sizes for bit in reversed(range(log2(size)))]

    def mine(self, i):
        axis, bit = self.names[i]
        return lax.rem(lax.axis_index(axis) // (1 << bit), 2)

    def partner(self, i):
        axis, bit = self.names[i]
        here = lax.axis_index(axis)
        return {axis: here + (1 << bit) * (1 - 2 * self.mine(i))}


def meet(partners):
    barrier = pltpu.get_barrier_semaphore()
    for device in partners:
        pl.semaphore_signal(barrier, inc=1, device_id=device, device_id_type=pl.DeviceIdType.MESH)
    pl.semaphore_wait(barrier, len(partners))


def gather_kernel(
    bits, orders, rel_ref, heads_ref, tails_ref, idx_ref,
    full_ref, hv_ref, tv_ref, nv_ref, heads_cat, tails_cat, send_sem, recv_sem,
):
    count = len(bits.names)
    parts = len(orders)
    rows = rel_ref.shape[0] // parts
    mine = [bits.mine(i) for i in range(count)]
    partner = [bits.partner(i) for i in range(count)]
    meet(partner)

    def start(part, stage):
        order = orders[part]
        done = set(order[:stage])
        where = tuple(slice(None) if i in done else mine[i] for i in range(count))
        where = where + (pl.ds(part * rows, rows),)
        source = rel_ref.at[pl.ds(part * rows, rows)] if stage == 0 else full_ref.at[where]
        copy = pltpu.make_async_remote_copy(
            src_ref=source,
            dst_ref=full_ref.at[where],
            send_sem=send_sem.at[part * count + stage],
            recv_sem=recv_sem.at[part * count + stage],
            device_id=partner[order[stage]],
            device_id_type=pl.DeviceIdType.MESH,
        )
        copy.start()
        return copy

    copies = [[start(part, 0)] for part in range(parts)]
    full_ref[tuple(mine)] = rel_ref[...]

    blocks, batch = idx_ref.shape[1], idx_ref.shape[2]
    width = heads_ref.shape[1]
    tile = 128

    def halves(source, cat):
        high, low = split(source[...])
        cat[:, :width] = high
        cat[:, width:] = low

    def take(which, b, cat, out):
        def body(t, carry):
            at = pl.ds(pl.multiple_of(t * tile, tile), tile)
            ids = idx_ref[which, b, at]
            hot = (ids == lax.broadcasted_iota(jnp.int32, (tile, cat.shape[0]), 1)).astype(BF16)
            both = dot(hot, cat[...], NN)
            out[b, at] = both[:, :width] + both[:, width:]
            return carry

        lax.fori_loop(0, batch // tile, body, 0)

    work = [lambda: (halves(heads_ref, heads_cat), halves(tails_ref, tails_cat))]
    work += [functools.partial(take, 0, b, heads_cat, hv_ref) for b in range(blocks)]
    work += [functools.partial(take, 1, b, tails_cat, tv_ref) for b in range(blocks)]
    work += [functools.partial(take, 2, b, tails_cat, nv_ref) for b in range(blocks)]
    per = -(-len(work) // count)
    for stage in range(count):
        for job in work[stage * per:(stage + 1) * per]:
            job()
        for part in range(parts):
            copies[part][stage].wait_recv()
            if stage + 1 < count:
                copies[part].append(start(part, stage + 1))
    for part in range(parts):
        for copy in copies[part]:
            copy.wait_send()


def compute_kernel(
    off_ref, rel_ref, hv_ref, tv_ref, nv_ref, idx_ref,
    head_ref, tail_ref, grad_ref,
    rel_hi, rel_lo, query, factor, through, spread,
):
    relations = off_ref.shape[1] - 1
    blocks, batch, width = hv_ref.shape
    negs = nv_ref.shape[1]
    window = 64
    row_id = lax.broadcasted_iota(jnp.int32, (window, 1), 0)

    def halve(r, carry):
        at = pl.ds(pl.multiple_of(r * width, width), width)
        rel_hi[at], rel_lo[at] = split(rel_ref[at])
        return carry

    lax.fori_loop(0, relations, halve, 0)
    query[...] = jnp.zeros_like(query)
    through[...] = jnp.zeros_like(through)

    def over_windows(step, after=None):
        def one(r, carry):
            low = [off_ref[b, r] for b in range(blocks)]
            high = [off_ref[b, r + 1] for b in range(blocks)]
            base = [low[b] // 8 * 8 for b in range(blocks)]
            trips = jnp.int32(0)
            for b in range(blocks):
                here = jnp.where(high[b] > low[b], (high[b] - base[b] + window - 1) // window, 0)
                trips = jnp.maximum(trips, here)
            at_r = pl.ds(pl.multiple_of(r * width, width), width)

            def inner(w, c):
                places, masks = [], []
                for b in range(blocks):
                    begin = base[b] + w * window
                    at = pl.multiple_of(jnp.minimum(begin, batch - window), 8)
                    first = jnp.maximum(low[b], begin)
                    last = jnp.minimum(high[b], begin + window)
                    ids = row_id + at
                    places.append(pl.ds(at, window))
                    masks.append(jnp.logical_and(ids >= first, ids < last))
                step(at_r, places, masks)
                return c

            lax.fori_loop(0, trips, inner, 0)
            return carry

        lax.fori_loop(0, relations, one, 0)

    def masked(ref, places, masks):
        return jnp.concatenate(
            [jnp.where(masks[b], ref[b, places[b]], 0.0) for b in range(blocks)], axis=0
        )

    def apply(source, out, dims):
        def step(at_r, places, masks):
            x = split(masked(source, places, masks))
            y = dot3(x, (rel_hi[at_r], rel_lo[at_r]), dims)
            for b in range(blocks):
                out[b, places[b]] += y[b * window:(b + 1) * window]
        return step

    over_windows(apply(hv_ref, query, NN))

    for b in range(blocks):
        q = query[b]
        tv = tv_ref[b]
        q2 = split(q)
        n2 = split(nv_ref[b])
        positive = jnp.sum(q * tv, axis=1, keepdims=True)
        coef = -jax.nn.sigmoid(-positive)
        weights = split(jax.nn.sigmoid(dot3(q2, n2, NT)) / negs)
        factor[b] = coef * tv + dot3(weights, n2, NN)
        rows = jnp.concatenate([coef * q, dot3(weights, q2, TN)], axis=0)
        high, low = split(rows)
        at = pl.ds(b * (batch + negs), batch + negs)
        spread[at, :width] = high
        spread[at, width:] = low

    grad_ref[...] = jnp.zeros_like(grad_ref)

    def outer(at_r, places, masks):
        x = split(masked(hv_ref, places, masks))
        f = split(jnp.concatenate([factor[b, places[b]] for b in range(blocks)], axis=0))
        grad_ref[at_r] += dot3(x, f, TN)

    over_windows(outer)
    over_windows(apply(factor, through, NT))

    tile = 256
    ids = idx_ref[1:2, :]

    def scatter(t, carry):
        at = pl.ds(pl.multiple_of(t * tile, tile), tile)
        hot = (ids == lax.broadcasted_iota(jnp.int32, (tile, ids.shape[1]), 0) + t * tile).astype(BF16)
        both = dot(hot, spread[...], NN)
        tail_ref[at] = both[:, :width] + both[:, width:]
        return carry

    lax.fori_loop(0, tail_ref.shape[0] // tile, scatter, 0)
    hids = idx_ref[0:1, :blocks * batch]
    hot = (hids == lax.broadcasted_iota(jnp.int32, (head_ref.shape[0], hids.shape[1]), 0)).astype(BF16)
    high, low = split(through[...].reshape(blocks * batch, width))
    head_ref[...] = dot(hot, high, NN) + dot(hot, low, NN)


def reduce_kernel(bits, plans, *refs):
    inputs = refs[:3]
    outs = refs[3:6]
    buffers = refs[6:-2]
    send_sem, recv_sem = refs[-2:]
    mine = [bits.mine(i) for i in range(len(bits.names))]
    partner = [bits.partner(i) for i in range(len(bits.names))]
    meet(partner)
    flows = []
    sem = 0
    buf = 0
    for array, order, part, parts in plans:
        rows = inputs[array].shape[-2] // parts
        flows.append(dict(
            array=array, order=order, rows=pl.ds(part * rows, rows), sem=sem,
            buffers=buffers[buf:buf + len(order)], left=sorted(order), copies=[],
        ))
        sem += len(order)
        buf += len(order)

    def cut(flow, stage, bit, value):
        place = flow["left"].index(bit)
        where = (slice(None),) * place + (value,)
        if stage == 0:
            where = where + (slice(None),) * (len(flow["left"]) - place - 1) + (flow["rows"],)
            return inputs[flow["array"]], where
        return flow["buffers"][stage - 1], where

    def start(flow, stage):
        bit = flow["order"][stage]
        ref, where = cut(flow, stage, bit, 1 - mine[bit])
        copy = pltpu.make_async_remote_copy(
            src_ref=ref.at[where],
            dst_ref=flow["buffers"][stage],
            send_sem=send_sem.at[flow["sem"] + stage],
            recv_sem=recv_sem.at[flow["sem"] + stage],
            device_id=partner[bit],
            device_id_type=pl.DeviceIdType.MESH,
        )
        copy.start()
        flow["copies"].append(copy)

    for flow in flows:
        start(flow, 0)
    for stage in range(max(len(flow["order"]) for flow in flows)):
        for flow in flows:
            order = flow["order"]
            if stage >= len(order):
                continue
            flow["copies"][stage].wait_recv()
            ref, where = cut(flow, stage, order[stage], mine[order[stage]])
            total = flow["buffers"][stage][...] + ref[where]
            flow["left"].remove(order[stage])
            if stage + 1 < len(order):
                flow["buffers"][stage][...] = total
                start(flow, stage + 1)
            else:
                outs[flow["array"]][flow["rows"]] = total
    for flow in flows:
        for copy in flow["copies"]:
            copy.wait_send()


def per_device(head_emb, tail_emb, relations, head_index, tail_index, rel_index, neg_index):
    heads_n, tails_n = lax.axis_size("head"), lax.axis_size("tail")
    width = relations.shape[1]
    own_rows = relations.shape[0]
    count_rel = own_rows * heads_n * tails_n // width
    heads, tails = head_emb[0], tail_emb[0]
    n_head, n_tail = heads.shape[0], tails.shape[0]
    steps, per_step, batch = head_index.shape[2:]
    negs = neg_index.shape[4]
    blocks = steps * per_step
    vmem = pl.BlockSpec(memory_space=pltpu.VMEM)

    local = [a[0, 0] for a in (head_index, tail_index, rel_index, neg_index)]
    per = [[] for _ in local]
    for s in range(steps):
        shift = s % tails_n
        rows = [a[s] for a in local]
        if shift:
            sent = jnp.concatenate([r.reshape(-1) for r in rows])
            sent = lax.ppermute(sent, "tail", [(i, (i - shift) % tails_n) for i in range(tails_n)])
            cuts, at = [], 0
            for r in rows:
                cuts.append(sent[at:at + r.size].reshape(r.shape))
                at += r.size
            rows = cuts
        for kept, r in zip(per, rows):
            kept.append(r)
    rows_h, rows_t, rows_r, rows_n = [jnp.concatenate(p, axis=0) for p in per]
    if count_rel * n_head * n_tail < 2 ** 31:
        keys = lax.sort((rows_r * n_head + rows_h) * n_tail + rows_t, dimension=1, is_stable=False)
        rows_t = keys % n_tail
        rows_h = (keys // n_tail) % n_head
        rows_r = keys // (n_tail * n_head)
    else:
        rows_r, rows_h, rows_t = lax.sort((rows_r, rows_h, rows_t), dimension=1, num_keys=1)
    bounds = jnp.arange(count_rel + 1, dtype=jnp.int32)
    offsets = jnp.sum((rows_r[:, None, :] < bounds[None, :, None]).astype(jnp.int32), axis=2)

    bits = Bits([("head", heads_n), ("tail", tails_n)])
    count = len(bits.names)
    hb, tb = log2(heads_n), log2(tails_n)
    head_bits, tail_bits = list(range(hb)), list(range(hb, hb + tb))
    core, planar = head_bits[-1:], head_bits[:-1]
    gather_orders = [tail_bits + planar + core, tail_bits + planar[::-1] + core]
    reduce_orders = [core + planar + tail_bits[::-1], core + planar[::-1] + tail_bits[::-1]]

    columns = jnp.stack([rows_h, rows_t, rows_n])[..., None]
    full, hv, tv, nv = pl.pallas_call(
        functools.partial(gather_kernel, bits, gather_orders),
        out_shape=(
            jax.ShapeDtypeStruct((2,) * count + (own_rows, width), F32),
            jax.ShapeDtypeStruct((blocks, batch, width), F32),
            jax.ShapeDtypeStruct((blocks, batch, width), F32),
            jax.ShapeDtypeStruct((blocks, negs, width), F32),
        ),
        in_specs=[vmem] * 4,
        out_specs=(vmem,) * 4,
        scratch_shapes=[
            pltpu.VMEM((n_head, 2 * width), BF16),
            pltpu.VMEM((n_tail, 2 * width), BF16),
            pltpu.SemaphoreType.DMA((2 * count,)),
            pltpu.SemaphoreType.DMA((2 * count,)),
        ],
        compiler_params=pltpu.CompilerParams(
            collective_id=0, has_side_effects=True, vmem_limit_bytes=VMEM_LIMIT
        ),
        name="gather",
    )(relations, heads, tails, columns)

    both = jnp.concatenate([rows_t, rows_n], axis=1).reshape(-1)
    lanes = jnp.stack([jnp.pad(rows_h.reshape(-1), (0, both.shape[0] - blocks * batch)), both])
    head_sum, tail_sum, rel_sum = pl.pallas_call(
        compute_kernel,
        out_shape=(
            jax.ShapeDtypeStruct((n_head, width), F32),
            jax.ShapeDtypeStruct((n_tail, width), F32),
            jax.ShapeDtypeStruct((count_rel * width, width), F32),
        ),
        in_specs=[pl.BlockSpec(memory_space=pltpu.SMEM)] + [vmem] * 5,
        out_specs=(vmem,) * 3,
        scratch_shapes=[
            pltpu.VMEM((count_rel * width, width), BF16),
            pltpu.VMEM((count_rel * width, width), BF16),
            pltpu.VMEM((blocks, batch, width), F32),
            pltpu.VMEM((blocks, batch, width), F32),
            pltpu.VMEM((blocks, batch, width), F32),
            pltpu.VMEM((blocks * (batch + negs), 2 * width), BF16),
        ],
        compiler_params=pltpu.CompilerParams(vmem_limit_bytes=VMEM_LIMIT),
        name="compute",
    )(offsets, full.reshape(count_rel * width, width), hv, tv, nv, lanes)

    plans = [(2, reduce_orders[0], 0, 2), (2, reduce_orders[1], 1, 2)]
    plans += [(1, core + planar, 0, 2), (1, core + planar[::-1], 1, 2)]
    plans += [(0, tail_bits[::-1], 0, 1)]
    inputs = (
        head_sum.reshape((2,) * tb + (n_head // tails_n, width)),
        tail_sum.reshape((2,) * hb + (n_tail // heads_n, width)),
        rel_sum.reshape((2,) * count + (own_rows, width)),
    )
    buffers, sems = [], 0
    for array, order, part, parts in plans:
        rows = inputs[array].shape[-2] // parts
        for stage in range(len(order)):
            buffers.append(pltpu.VMEM((2,) * (len(order) - 1 - stage) + (rows, width), F32))
        sems += len(order)
    head_share, tail_share, rel_share = pl.pallas_call(
        functools.partial(reduce_kernel, bits, plans),
        out_shape=tuple(jax.ShapeDtypeStruct(a.shape[-2:], F32) for a in inputs),
        in_specs=[vmem] * 3,
        out_specs=(vmem,) * 3,
        scratch_shapes=buffers + [pltpu.SemaphoreType.DMA((sems,)), pltpu.SemaphoreType.DMA((sems,))],
        compiler_params=pltpu.CompilerParams(
            collective_id=1, has_side_effects=True, vmem_limit_bytes=VMEM_LIMIT
        ),
        name="reduce",
    )(*inputs)
    return (head_share[None], tail_share[None], rel_share)


def solution(mesh):
    placed = (
        P("head", None, None),
        P("tail", None, None),
        P(("head", "tail"), None),
        P("head", "tail", None, None, None),
        P("head", "tail", None, None, None),
        P("head", "tail", None, None, None),
        P("head", "tail", None, None, None),
    )
    return jax.shard_map(
        per_device,
        mesh=mesh,
        in_specs=placed,
        out_specs=(P("head", "tail", None), P("tail", "head", None), P(("head", "tail"), None)),
        check_vma=False,
    )
```

```python
import functools
import jax
import jax.numpy as jnp
from jax import lax
from jax.experimental import pallas as pl
from jax.experimental.pallas import tpu as pltpu
from jax.sharding import PartitionSpec as P

F32 = jnp.float32
BF16 = jnp.bfloat16
VMEM_LIMIT = 60 * 1024 * 1024
GROUPS = 2
NN = (((1,), (0,)), ((), ()))
NT = (((1,), (1,)), ((), ()))
TN = (((0,), (0,)), ((), ()))


def split(x):
    high = x.astype(BF16)
    return high, (x - high.astype(F32)).astype(BF16)


def dot(a, b, dims):
    return lax.dot_general(a, b, dims, preferred_element_type=F32)


def dot3(a, b, dims):
    return dot(a[0], b[0], dims) + (dot(a[0], b[1], dims) + dot(a[1], b[0], dims))


def log2(n):
    assert n & (n - 1) == 0
    return n.bit_length() - 1


class Bits:
    def __init__(self, sizes):
        self.names = [(axis, bit) for axis, size in sizes for bit in reversed(range(log2(size)))]

    def mine(self, i):
        axis, bit = self.names[i]
        return lax.rem(lax.axis_index(axis) // (1 << bit), 2)

    def partner(self, i):
        axis, bit = self.names[i]
        here = lax.axis_index(axis)
        return {axis: here + (1 << bit) * (1 - 2 * self.mine(i))}


def meet(partners):
    barrier = pltpu.get_barrier_semaphore()
    for device in partners:
        pl.semaphore_signal(barrier, inc=1, device_id=device, device_id_type=pl.DeviceIdType.MESH)
    pl.semaphore_wait(barrier, len(partners))


def column(row):
    return jnp.transpose(jnp.broadcast_to(row, (8, row.shape[1])))[:, :1]


def gather_kernel(
    bits, orders, tails_n, steps, count_rel, *refs,
):
    rel_ref, heads_ref, tails_ref = refs[:3]
    sent_idx = refs[3:7]
    full_ref, hv_ref, tv_ref, nv_ref, off_ref, head_ids, tail_ids = refs[7:14]
    heads_cat, tails_cat, cols, neg_cols = refs[14:18]
    got_idx = refs[18:22]
    send_sem, recv_sem, idx_send, idx_recv = refs[22:]
    count = len(bits.names)
    parts = len(orders)
    rows = rel_ref.shape[0] // parts
    mine = [bits.mine(i) for i in range(count)]
    partner = [bits.partner(i) for i in range(count)]
    blocks, batch = hv_ref.shape[:2]
    negs = nv_ref.shape[1]
    per_step = blocks // steps
    width = heads_ref.shape[1]

    me = lax.axis_index("tail")
    around, moves = [], []
    for s in range(steps):
        if s % tails_n:
            to = {"tail": lax.rem(me + tails_n - s % tails_n, tails_n)}
            around += [to, {"tail": lax.rem(me + s % tails_n, tails_n)}]
            moves.append((s, to))
    meet(partner + around)
    idx_copies = []
    for s, to in moves:
        for a in range(4):
            at = pl.ds(s * per_step, per_step)
            sem = len(idx_copies)
            copy = pltpu.make_async_remote_copy(
                src_ref=sent_idx[a].at[at],
                dst_ref=got_idx[a].at[at],
                send_sem=idx_send.at[sem],
                recv_sem=idx_recv.at[sem],
                device_id=to,
                device_id_type=pl.DeviceIdType.MESH,
            )
            copy.start()
            idx_copies.append(copy)

    def start(part, stage):
        order = orders[part]
        done = set(order[:stage])
        where = tuple(slice(None) if i in done else mine[i] for i in range(count))
        where = where + (pl.ds(part * rows, rows),)
        source = rel_ref.at[pl.ds(part * rows, rows)] if stage == 0 else full_ref.at[where]
        copy = pltpu.make_async_remote_copy(
            src_ref=source,
            dst_ref=full_ref.at[where],
            send_sem=send_sem.at[part * count + stage],
            recv_sem=recv_sem.at[part * count + stage],
            device_id=partner[order[stage]],
            device_id_type=pl.DeviceIdType.MESH,
        )
        copy.start()
        return copy

    copies = [[start(part, 0)] for part in range(parts)]
    full_ref[tuple(mine)] = rel_ref[...]

    def halves(source, cat):
        high, low = split(source[...])
        cat[:, :width] = high
        cat[:, width:] = low

    def arrive():
        for copy in idx_copies:
            copy.wait_recv()

    def order_block(b):
        moved = (b // per_step) % tails_n != 0
        row = [(got_idx if moved else sent_idx)[a][b] for a in range(4)]
        rel = column(row[2])
        lanes = off_ref.shape[2]
        lane = lax.broadcasted_iota(jnp.int32, (batch, lanes), 1)
        base = jnp.sum((rel < lane).astype(jnp.int32), axis=0, keepdims=True)
        off_ref[b] = base
        same = rel == lane
        earlier = (
            lax.broadcasted_iota(jnp.int32, (batch, batch), 1)
            < lax.broadcasted_iota(jnp.int32, (batch, batch), 0)
        ).astype(BF16)
        rank = dot(earlier, same.astype(BF16), NN).astype(jnp.int32)
        place = jnp.sum(jnp.where(same, rank + base, 0), axis=1, keepdims=True)
        to = place == lax.broadcasted_iota(jnp.int32, (batch, batch), 1)
        ids = [jnp.sum(jnp.where(to, column(row[a]), 0), axis=0, keepdims=True) for a in (0, 1)]
        head_ids[b] = ids[0]
        tail_ids[:, b * (batch + negs):b * (batch + negs) + batch] = ids[1]
        tail_ids[:, b * (batch + negs) + batch:(b + 1) * (batch + negs)] = row[3]
        cols[0, b] = column(ids[0])
        cols[1, b] = column(ids[1])
        neg_cols[0, b] = column(row[3])

    def take(source, which, b, cat, out):
        tile = 128

        def body(t, carry):
            at = pl.ds(pl.multiple_of(t * tile, tile), tile)
            ids = source[which, b, at]
            hot = (ids == lax.broadcasted_iota(jnp.int32, (tile, cat.shape[0]), 1)).astype(BF16)
            both = dot(hot, cat[...], NN)
            out[b, at] = both[:, :width] + both[:, width:]
            return carry

        lax.fori_loop(0, out.shape[1] // tile, body, 0)

    work = [lambda: (halves(heads_ref, heads_cat), halves(tails_ref, tails_cat)), arrive]
    work += [functools.partial(order_block, b) for b in range(blocks)]
    work += [functools.partial(take, cols, 0, b, heads_cat, hv_ref) for b in range(blocks)]
    work += [functools.partial(take, cols, 1, b, tails_cat, tv_ref) for b in range(blocks)]
    work += [functools.partial(take, neg_cols, 0, b, tails_cat, nv_ref) for b in range(blocks)]
    groups = parts // 2
    total = count * groups
    done = 0
    turn = 0
    for step in range(count + groups - 1):
        for group in range(groups):
            stage = step - group
            if not 0 <= stage < count:
                continue
            turn += 1
            upto = -(-len(work) * turn // total)
            for job in work[done:upto]:
                job()
            done = upto
            for part in (2 * group, 2 * group + 1):
                copies[part][stage].wait_recv()
                if stage + 1 < count:
                    copies[part].append(start(part, stage + 1))
    for copy in idx_copies:
        copy.wait_send()
    for part in range(parts):
        for copy in copies[part]:
            copy.wait_send()


def compute_kernel(
    relations, off_ref, rel_ref, hv_ref, tv_ref, nv_ref,
    back_ref, spread, grad_ref,
    rel_hi, rel_lo, query, factor, through,
):
    blocks, batch, width = hv_ref.shape
    negs = nv_ref.shape[1]
    window = 64
    row_id = lax.broadcasted_iota(jnp.int32, (window, 1), 0)

    def halve(r, carry):
        at = pl.ds(pl.multiple_of(r * width, width), width)
        rel_hi[at], rel_lo[at] = split(rel_ref[at])
        return carry

    lax.fori_loop(0, relations, halve, 0)
    query[...] = jnp.zeros_like(query)
    through[...] = jnp.zeros_like(through)

    def over_windows(step, after=None):
        def one(r, carry):
            low = [off_ref[b, 0, r] for b in range(blocks)]
            high = [off_ref[b, 0, r + 1] for b in range(blocks)]
            base = [low[b] // 8 * 8 for b in range(blocks)]
            trips = jnp.int32(0)
            for b in range(blocks):
                here = jnp.where(high[b] > low[b], (high[b] - base[b] + window - 1) // window, 0)
                trips = jnp.maximum(trips, here)
            at_r = pl.ds(pl.multiple_of(r * width, width), width)

            def inner(w, c):
                places, masks = [], []
                for b in range(blocks):
                    begin = base[b] + w * window
                    at = pl.multiple_of(jnp.minimum(begin, batch - window), 8)
                    first = jnp.maximum(low[b], begin)
                    last = jnp.minimum(high[b], begin + window)
                    ids = row_id + at
                    places.append(pl.ds(at, window))
                    masks.append(jnp.logical_and(ids >= first, ids < last))
                step(at_r, places, masks)
                return c

            lax.fori_loop(0, trips, inner, 0)
            return carry

        lax.fori_loop(0, relations, one, 0)

    def masked(ref, places, masks):
        return jnp.concatenate(
            [jnp.where(masks[b], ref[b, places[b]], 0.0) for b in range(blocks)], axis=0
        )

    def apply(source, out, dims):
        def step(at_r, places, masks):
            x = split(masked(source, places, masks))
            y = dot3(x, (rel_hi[at_r], rel_lo[at_r]), dims)
            for b in range(blocks):
                out[b, places[b]] += y[b * window:(b + 1) * window]
        return step

    over_windows(apply(hv_ref, query, NN))

    for b in range(blocks):
        q = query[b]
        tv = tv_ref[b]
        q2 = split(q)
        n2 = split(nv_ref[b])
        positive = jnp.sum(q * tv, axis=1, keepdims=True)
        coef = -jax.nn.sigmoid(-positive)
        weights = split(jax.nn.sigmoid(dot3(q2, n2, NT)) / negs)
        factor[b] = coef * tv + dot3(weights, n2, NN)
        rows = jnp.concatenate([coef * q, dot3(weights, q2, TN)], axis=0)
        high, low = split(rows)
        at = pl.ds(b * (batch + negs), batch + negs)
        spread[at, :width] = high
        spread[at, width:] = low

    grad_ref[...] = jnp.zeros_like(grad_ref)

    def outer(at_r, places, masks):
        x = split(masked(hv_ref, places, masks))
        f = split(jnp.concatenate([factor[b, places[b]] for b in range(blocks)], axis=0))
        grad_ref[at_r] += dot3(x, f, TN)

    over_windows(outer)
    over_windows(apply(factor, through, NT))

    for b in range(blocks):
        high, low = split(through[b])
        back_ref[pl.ds(b * batch, batch), :width] = high
        back_ref[pl.ds(b * batch, batch), width:] = low


def reduce_kernel(bits, plans, grad_ref, spread, back, tail_ids, head_ids, *refs):
    outs = refs[:3]
    head_sum, tail_sum = refs[3:5]
    buffers = refs[5:-2]
    send_sem, recv_sem = refs[-2:]
    inputs = (head_sum, tail_sum, grad_ref)
    width = grad_ref.shape[-1]
    mine = [bits.mine(i) for i in range(len(bits.names))]
    partner = [bits.partner(i) for i in range(len(bits.names))]
    meet(partner)
    flows = []
    sem = 0
    buf = 0
    for array, order, part, parts, group in plans:
        rows = inputs[array].shape[-2] // parts
        flows.append(dict(
            array=array, order=order, rows=pl.ds(part * rows, rows), sem=sem, group=group,
            buffers=buffers[buf:buf + len(order)], left=sorted(order), copies=[],
        ))
        sem += len(order)
        buf += len(order)

    def cut(flow, stage, bit, value):
        place = flow["left"].index(bit)
        where = (slice(None),) * place + (value,)
        if stage == 0:
            where = where + (slice(None),) * (len(flow["left"]) - place - 1) + (flow["rows"],)
            return inputs[flow["array"]], where
        return flow["buffers"][stage - 1], where

    def start(flow, stage):
        bit = flow["order"][stage]
        ref, where = cut(flow, stage, bit, 1 - mine[bit])
        copy = pltpu.make_async_remote_copy(
            src_ref=ref.at[where],
            dst_ref=flow["buffers"][stage],
            send_sem=send_sem.at[flow["sem"] + stage],
            recv_sem=recv_sem.at[flow["sem"] + stage],
            device_id=partner[bit],
            device_id_type=pl.DeviceIdType.MESH,
        )
        copy.start()
        flow["copies"].append(copy)

    def begin(array):
        for flow in flows:
            if flow["array"] == array:
                start(flow, 0)

    def scatter(ids, source, out):
        dims = len(out.shape) - 2
        rows = out.shape[-2]

        def body(t, carry):
            hot = (ids == lax.broadcasted_iota(jnp.int32, (rows, ids.shape[1]), 0) + t * rows)
            both = dot(hot.astype(BF16), source[...], NN)
            where = tuple(lax.rem(t // (1 << i), 2) for i in reversed(range(dims)))
            out[where] = both[:, :width] + both[:, width:]
            return carry

        lax.fori_loop(0, 1 << dims, body, 0)

    begin(2)
    heads = jnp.concatenate([head_ids[b] for b in range(head_ids.shape[0])], axis=1)
    scatter(heads, back, head_sum)
    begin(0)
    scatter(tail_ids[...], spread, tail_sum)
    begin(1)
    groups = 1 + max(flow["group"] for flow in flows)
    for step in range(len(bits.names) + groups - 1):
        for flow in flows:
            order = flow["order"]
            stage = step - flow["group"]
            if not 0 <= stage < len(order):
                continue
            flow["copies"][stage].wait_recv()
            ref, where = cut(flow, stage, order[stage], mine[order[stage]])
            total = flow["buffers"][stage][...] + ref[where]
            flow["left"].remove(order[stage])
            if stage + 1 < len(order):
                flow["buffers"][stage][...] = total
                start(flow, stage + 1)
            else:
                outs[flow["array"]][flow["rows"]] = total
    for flow in flows:
        for copy in flow["copies"]:
            copy.wait_send()


def finish_kernel(*refs):
    for source, out in zip(refs[:3], refs[3:]):
        out[...] = source[...]


def per_device(head_emb, tail_emb, relations, head_index, tail_index, rel_index, neg_index):
    heads_n, tails_n = lax.axis_size("head"), lax.axis_size("tail")
    width = relations.shape[1]
    own_rows = relations.shape[0]
    count_rel = own_rows * heads_n * tails_n // width
    heads, tails = head_emb[0], tail_emb[0]
    n_head, n_tail = heads.shape[0], tails.shape[0]
    steps, per_step, batch = head_index.shape[2:]
    negs = neg_index.shape[4]
    blocks = steps * per_step
    each = batch + negs
    lanes = (count_rel + 128) // 128 * 128
    vmem = pl.BlockSpec(memory_space=pltpu.VMEM)
    shape = jax.ShapeDtypeStruct

    bits = Bits([("head", heads_n), ("tail", tails_n)])
    count = len(bits.names)
    hb, tb = log2(heads_n), log2(tails_n)
    head_bits, tail_bits = list(range(hb)), list(range(hb, hb + tb))
    core, planar = head_bits[-1:], head_bits[:-1]
    groups = min(GROUPS, own_rows // 16)
    gather_orders = [tail_bits + planar + core, tail_bits + planar[::-1] + core] * groups
    reduce_orders = [core + planar + tail_bits[::-1], core + planar[::-1] + tail_bits[::-1]]

    indices = [
        a.reshape(blocks, 1, a.shape[-1]) for a in (head_index, tail_index, rel_index, neg_index)
    ]
    full, hv, tv, nv, offsets, head_ids, tail_ids = pl.pallas_call(
        functools.partial(gather_kernel, bits, gather_orders, tails_n, steps, count_rel),
        out_shape=(
            shape((2,) * count + (own_rows, width), F32),
            shape((blocks, batch, width), F32),
            shape((blocks, batch, width), F32),
            shape((blocks, negs, width), F32),
            shape((blocks, 1, lanes), jnp.int32),
            shape((blocks, 1, batch), jnp.int32),
            shape((1, blocks * each), jnp.int32),
        ),
        in_specs=[vmem] * 7,
        out_specs=(vmem,) * 7,
        scratch_shapes=[
            pltpu.VMEM((n_head, 2 * width), BF16),
            pltpu.VMEM((n_tail, 2 * width), BF16),
            pltpu.VMEM((2, blocks, batch, 1), jnp.int32),
            pltpu.VMEM((1, blocks, negs, 1), jnp.int32),
        ] + [pltpu.VMEM(a.shape, jnp.int32) for a in indices] + [
            pltpu.SemaphoreType.DMA((len(gather_orders) * count,)),
            pltpu.SemaphoreType.DMA((len(gather_orders) * count,)),
            pltpu.SemaphoreType.DMA((4 * steps,)),
            pltpu.SemaphoreType.DMA((4 * steps,)),
        ],
        compiler_params=pltpu.CompilerParams(
            collective_id=0, has_side_effects=True, vmem_limit_bytes=VMEM_LIMIT
        ),
        name="gather",
    )(relations, heads, tails, *indices)

    back, spread, rel_sum = pl.pallas_call(
        functools.partial(compute_kernel, count_rel),
        out_shape=(
            shape((blocks * batch, 2 * width), BF16),
            shape((blocks * each, 2 * width), BF16),
            shape((count_rel * width, width), F32),
        ),
        in_specs=[pl.BlockSpec(memory_space=pltpu.SMEM)] + [vmem] * 4,
        out_specs=(vmem,) * 3,
        scratch_shapes=[
            pltpu.VMEM((count_rel * width, width), BF16),
            pltpu.VMEM((count_rel * width, width), BF16),
            pltpu.VMEM((blocks, batch, width), F32),
            pltpu.VMEM((blocks, batch, width), F32),
            pltpu.VMEM((blocks, batch, width), F32),
        ],
        compiler_params=pltpu.CompilerParams(vmem_limit_bytes=VMEM_LIMIT),
        name="compute",
    )(offsets, full.reshape(count_rel * width, width), hv, tv, nv)

    sizes = (
        (2,) * tb + (n_head // tails_n, width),
        (2,) * hb + (n_tail // heads_n, width),
        (2,) * count + (own_rows, width),
    )
    plans = []
    for group in range(groups):
        plans += [(2, reduce_orders[i], 2 * group + i, 2 * groups, group) for i in range(2)]
        plans += [
            (1, (core + planar, core + planar[::-1])[i], 2 * group + i, 2 * groups, group)
            for i in range(2)
        ]
    plans += [(0, tail_bits[::-1], 0, 1, 0)]
    buffers, sems = [], 0
    for array, order, part, parts, group in plans:
        rows = sizes[array][-2] // parts
        for stage in range(len(order)):
            buffers.append(pltpu.VMEM((2,) * (len(order) - 1 - stage) + (rows, width), F32))
        sems += len(order)
    shares = tuple(shape(a[-2:], F32) for a in sizes)
    totals = pl.pallas_call(
        functools.partial(reduce_kernel, bits, plans),
        out_shape=shares,
        in_specs=[vmem] * 5,
        out_specs=(vmem,) * 3,
        scratch_shapes=[pltpu.VMEM(sizes[0], F32), pltpu.VMEM(sizes[1], F32)] + buffers
        + [pltpu.SemaphoreType.DMA((sems,)), pltpu.SemaphoreType.DMA((sems,))],
        compiler_params=pltpu.CompilerParams(
            collective_id=1, has_side_effects=True, vmem_limit_bytes=VMEM_LIMIT
        ),
        name="reduce",
    )(rel_sum.reshape(sizes[2]), spread, back, tail_ids, head_ids)
    head_share, tail_share, rel_share = pl.pallas_call(
        finish_kernel,
        out_shape=shares,
        in_specs=[vmem] * 3,
        out_specs=(vmem,) * 3,
        name="finish",
    )(*totals)
    return (head_share[None], tail_share[None], rel_share)


def solution(mesh):
    placed = (
        P("head", None, None),
        P("tail", None, None),
        P(("head", "tail"), None),
        P("head", "tail", None, None, None),
        P("head", "tail", None, None, None),
        P("head", "tail", None, None, None),
        P("head", "tail", None, None, None),
    )
    return jax.shard_map(
        per_device,
        mesh=mesh,
        in_specs=placed,
        out_specs=(P("head", "tail", None), P("tail", "head", None), P(("head", "tail"), None)),
        check_vma=False,
    )
```

```python
import functools
import jax
import jax.numpy as jnp
from jax import lax
from jax.experimental import pallas as pl
from jax.experimental.pallas import tpu as pltpu
from jax.sharding import PartitionSpec as P

F32 = jnp.float32
BF16 = jnp.bfloat16
VMEM_LIMIT = 60 * 1024 * 1024
GATHER_EARLY = 0.375
REDUCE_EARLY = 0.375
NN = (((1,), (0,)), ((), ()))
NT = (((1,), (1,)), ((), ()))
TN = (((0,), (0,)), ((), ()))


def split(x):
    high = x.astype(BF16)
    return high, (x - high.astype(F32)).astype(BF16)


def dot(a, b, dims):
    return lax.dot_general(a, b, dims, preferred_element_type=F32)


def dot3(a, b, dims):
    return dot(a[0], b[0], dims) + (dot(a[0], b[1], dims) + dot(a[1], b[0], dims))


def log2(n):
    assert n & (n - 1) == 0
    return n.bit_length() - 1


class Bits:
    def __init__(self, sizes):
        self.names = [(axis, bit) for axis, size in sizes for bit in reversed(range(log2(size)))]

    def mine(self, i):
        axis, bit = self.names[i]
        return lax.rem(lax.axis_index(axis) // (1 << bit), 2)

    def partner(self, i):
        axis, bit = self.names[i]
        here = lax.axis_index(axis)
        return {axis: here + (1 << bit) * (1 - 2 * self.mine(i))}


def share(rows, early, orders):
    small = max(8, int(rows * early / 16) * 8)
    big = rows // 2 - small
    cuts, first = [], 0
    for order, size in zip(orders, (big, big, small, small)):
        cuts.append((order, first, size))
        first += size
    return cuts


def meet(partners):
    barrier = pltpu.get_barrier_semaphore()
    for device in partners:
        pl.semaphore_signal(barrier, inc=1, device_id=device, device_id_type=pl.DeviceIdType.MESH)
    pl.semaphore_wait(barrier, len(partners))


def column(row):
    return jnp.transpose(jnp.broadcast_to(row, (8, row.shape[1])))[:, :1]


def gather_kernel(
    bits, orders, tails_n, steps, count_rel, *refs,
):
    rel_ref, heads_ref, tails_ref = refs[:3]
    sent_idx = refs[3:7]
    full_ref, hv_ref, tv_ref, nv_ref, off_ref, head_ids, tail_ids = refs[7:14]
    heads_cat, tails_cat, cols, neg_cols = refs[14:18]
    got_idx = refs[18:22]
    send_sem, recv_sem, idx_send, idx_recv = refs[22:]
    count = len(bits.names)
    parts = len(orders)
    mine = [bits.mine(i) for i in range(count)]
    partner = [bits.partner(i) for i in range(count)]
    blocks, batch = hv_ref.shape[:2]
    negs = nv_ref.shape[1]
    per_step = blocks // steps
    width = heads_ref.shape[1]

    me = lax.axis_index("tail")
    around, moves = [], []
    for s in range(steps):
        if s % tails_n:
            to = {"tail": lax.rem(me + tails_n - s % tails_n, tails_n)}
            around += [to, {"tail": lax.rem(me + s % tails_n, tails_n)}]
            moves.append((s, to))
    meet(partner + around)
    idx_copies = []
    for s, to in moves:
        for a in range(4):
            at = pl.ds(s * per_step, per_step)
            sem = len(idx_copies)
            copy = pltpu.make_async_remote_copy(
                src_ref=sent_idx[a].at[at],
                dst_ref=got_idx[a].at[at],
                send_sem=idx_send.at[sem],
                recv_sem=idx_recv.at[sem],
                device_id=to,
                device_id_type=pl.DeviceIdType.MESH,
            )
            copy.start()
            idx_copies.append(copy)

    def start(part, stage):
        order, first, rows = orders[part]
        done = set(order[:stage])
        where = tuple(slice(None) if i in done else mine[i] for i in range(count))
        where = where + (pl.ds(first, rows),)
        source = rel_ref.at[pl.ds(first, rows)] if stage == 0 else full_ref.at[where]
        copy = pltpu.make_async_remote_copy(
            src_ref=source,
            dst_ref=full_ref.at[where],
            send_sem=send_sem.at[part * count + stage],
            recv_sem=recv_sem.at[part * count + stage],
            device_id=partner[order[stage]],
            device_id_type=pl.DeviceIdType.MESH,
        )
        copy.start()
        return copy

    copies = [[start(part, 0)] for part in range(parts)]
    full_ref[tuple(mine)] = rel_ref[...]

    def halves(source, cat):
        high, low = split(source[...])
        cat[:, :width] = high
        cat[:, width:] = low

    def arrive():
        for copy in idx_copies:
            copy.wait_recv()

    def order_block(b):
        moved = (b // per_step) % tails_n != 0
        row = [(got_idx if moved else sent_idx)[a][b] for a in range(4)]
        rel = column(row[2])
        lanes = off_ref.shape[2]
        lane = lax.broadcasted_iota(jnp.int32, (batch, lanes), 1)
        base = jnp.sum((rel < lane).astype(jnp.int32), axis=0, keepdims=True)
        off_ref[b] = base
        same = rel == lane
        earlier = (
            lax.broadcasted_iota(jnp.int32, (batch, batch), 1)
            < lax.broadcasted_iota(jnp.int32, (batch, batch), 0)
        ).astype(BF16)
        rank = dot(earlier, same.astype(BF16), NN).astype(jnp.int32)
        place = jnp.sum(jnp.where(same, rank + base, 0), axis=1, keepdims=True)
        to = place == lax.broadcasted_iota(jnp.int32, (batch, batch), 1)
        ids = [jnp.sum(jnp.where(to, column(row[a]), 0), axis=0, keepdims=True) for a in (0, 1)]
        head_ids[b] = ids[0]
        tail_ids[:, b * (batch + negs):b * (batch + negs) + batch] = ids[1]
        tail_ids[:, b * (batch + negs) + batch:(b + 1) * (batch + negs)] = row[3]
        cols[0, b] = column(ids[0])
        cols[1, b] = column(ids[1])
        neg_cols[0, b] = column(row[3])

    def take(source, which, b, cat, out):
        tile = 128

        def body(t, carry):
            at = pl.ds(pl.multiple_of(t * tile, tile), tile)
            ids = source[which, b, at]
            hot = (ids == lax.broadcasted_iota(jnp.int32, (tile, cat.shape[0]), 1)).astype(BF16)
            both = dot(hot, cat[...], NN)
            out[b, at] = both[:, :width] + both[:, width:]
            return carry

        lax.fori_loop(0, out.shape[1] // tile, body, 0)

    work = [lambda: (halves(heads_ref, heads_cat), halves(tails_ref, tails_cat)), arrive]
    work += [functools.partial(order_block, b) for b in range(blocks)]
    work += [functools.partial(take, cols, 0, b, heads_cat, hv_ref) for b in range(blocks)]
    work += [functools.partial(take, cols, 1, b, tails_cat, tv_ref) for b in range(blocks)]
    work += [functools.partial(take, neg_cols, 0, b, tails_cat, nv_ref) for b in range(blocks)]
    done = 0
    for stage in range(count):
        upto = -(-len(work) * (stage + 1) // count)
        for job in work[done:upto]:
            job()
        done = upto
        for part in range(parts):
            copies[part][stage].wait_recv()
            if stage + 1 < count:
                copies[part].append(start(part, stage + 1))
    for copy in idx_copies:
        copy.wait_send()
    for part in range(parts):
        for copy in copies[part]:
            copy.wait_send()


def compute_kernel(
    relations, off_ref, rel_ref, hv_ref, tv_ref, nv_ref,
    back_ref, spread, grad_ref,
    rel_hi, rel_lo, query, factor, through,
):
    blocks, batch, width = hv_ref.shape
    negs = nv_ref.shape[1]
    window = 64
    row_id = lax.broadcasted_iota(jnp.int32, (window, 1), 0)

    def halve(r, carry):
        at = pl.ds(pl.multiple_of(r * width, width), width)
        rel_hi[at], rel_lo[at] = split(rel_ref[at])
        return carry

    lax.fori_loop(0, relations, halve, 0)
    query[...] = jnp.zeros_like(query)
    through[...] = jnp.zeros_like(through)

    def over_windows(step, after=None):
        def one(r, carry):
            low = [off_ref[b, 0, r] for b in range(blocks)]
            high = [off_ref[b, 0, r + 1] for b in range(blocks)]
            base = [low[b] // 8 * 8 for b in range(blocks)]
            trips = jnp.int32(0)
            for b in range(blocks):
                here = jnp.where(high[b] > low[b], (high[b] - base[b] + window - 1) // window, 0)
                trips = jnp.maximum(trips, here)
            at_r = pl.ds(pl.multiple_of(r * width, width), width)

            def inner(w, c):
                places, masks = [], []
                for b in range(blocks):
                    begin = base[b] + w * window
                    at = pl.multiple_of(jnp.minimum(begin, batch - window), 8)
                    first = jnp.maximum(low[b], begin)
                    last = jnp.minimum(high[b], begin + window)
                    ids = row_id + at
                    places.append(pl.ds(at, window))
                    masks.append(jnp.logical_and(ids >= first, ids < last))
                step(at_r, places, masks)
                return c

            lax.fori_loop(0, trips, inner, 0)
            return carry

        lax.fori_loop(0, relations, one, 0)

    def masked(ref, places, masks):
        return jnp.concatenate(
            [jnp.where(masks[b], ref[b, places[b]], 0.0) for b in range(blocks)], axis=0
        )

    def apply(source, out, dims):
        def step(at_r, places, masks):
            x = split(masked(source, places, masks))
            y = dot3(x, (rel_hi[at_r], rel_lo[at_r]), dims)
            for b in range(blocks):
                out[b, places[b]] += y[b * window:(b + 1) * window]
        return step

    over_windows(apply(hv_ref, query, NN))

    for b in range(blocks):
        q = query[b]
        tv = tv_ref[b]
        q2 = split(q)
        n2 = split(nv_ref[b])
        positive = jnp.sum(q * tv, axis=1, keepdims=True)
        coef = -jax.nn.sigmoid(-positive)
        weights = split(jax.nn.sigmoid(dot3(q2, n2, NT)) / negs)
        factor[b] = coef * tv + dot3(weights, n2, NN)
        rows = jnp.concatenate([coef * q, dot3(weights, q2, TN)], axis=0)
        high, low = split(rows)
        at = pl.ds(b * (batch + negs), batch + negs)
        spread[at, :width] = high
        spread[at, width:] = low

    grad_ref[...] = jnp.zeros_like(grad_ref)

    def outer(at_r, places, masks):
        x = split(masked(hv_ref, places, masks))
        f = split(jnp.concatenate([factor[b, places[b]] for b in range(blocks)], axis=0))
        grad_ref[at_r] += dot3(x, f, TN)

    over_windows(outer)
    over_windows(apply(factor, through, NT))

    for b in range(blocks):
        high, low = split(through[b])
        back_ref[pl.ds(b * batch, batch), :width] = high
        back_ref[pl.ds(b * batch, batch), width:] = low


def reduce_kernel(bits, plans, grad_ref, spread, back, tail_ids, head_ids, *refs):
    outs = refs[:3]
    head_sum, tail_sum = refs[3:5]
    buffers = refs[5:-2]
    send_sem, recv_sem = refs[-2:]
    inputs = (head_sum, tail_sum, grad_ref)
    width = grad_ref.shape[-1]
    mine = [bits.mine(i) for i in range(len(bits.names))]
    partner = [bits.partner(i) for i in range(len(bits.names))]
    meet(partner)
    flows = []
    sem = 0
    buf = 0
    for array, order, first, rows in plans:
        flows.append(dict(
            array=array, order=order, rows=pl.ds(first, rows), sem=sem,
            buffers=buffers[buf:buf + len(order)], left=sorted(order), copies=[],
        ))
        sem += len(order)
        buf += len(order)

    def cut(flow, stage, bit, value):
        place = flow["left"].index(bit)
        where = (slice(None),) * place + (value,)
        if stage == 0:
            where = where + (slice(None),) * (len(flow["left"]) - place - 1) + (flow["rows"],)
            return inputs[flow["array"]], where
        return flow["buffers"][stage - 1], where

    def start(flow, stage):
        bit = flow["order"][stage]
        ref, where = cut(flow, stage, bit, 1 - mine[bit])
        copy = pltpu.make_async_remote_copy(
            src_ref=ref.at[where],
            dst_ref=flow["buffers"][stage],
            send_sem=send_sem.at[flow["sem"] + stage],
            recv_sem=recv_sem.at[flow["sem"] + stage],
            device_id=partner[bit],
            device_id_type=pl.DeviceIdType.MESH,
        )
        copy.start()
        flow["copies"].append(copy)

    def begin(array):
        for flow in flows:
            if flow["array"] == array:
                start(flow, 0)

    def scatter(ids, source, out):
        dims = len(out.shape) - 2
        rows = out.shape[-2]

        def body(t, carry):
            hot = (ids == lax.broadcasted_iota(jnp.int32, (rows, ids.shape[1]), 0) + t * rows)
            both = dot(hot.astype(BF16), source[...], NN)
            where = tuple(lax.rem(t // (1 << i), 2) for i in reversed(range(dims)))
            out[where] = both[:, :width] + both[:, width:]
            return carry

        lax.fori_loop(0, 1 << dims, body, 0)

    begin(2)
    heads = jnp.concatenate([head_ids[b] for b in range(head_ids.shape[0])], axis=1)
    scatter(heads, back, head_sum)
    begin(0)
    scatter(tail_ids[...], spread, tail_sum)
    begin(1)
    for stage in range(len(bits.names)):
        for flow in flows:
            order = flow["order"]
            if stage >= len(order):
                continue
            flow["copies"][stage].wait_recv()
            ref, where = cut(flow, stage, order[stage], mine[order[stage]])
            total = flow["buffers"][stage][...] + ref[where]
            flow["left"].remove(order[stage])
            if stage + 1 < len(order):
                flow["buffers"][stage][...] = total
                start(flow, stage + 1)
            else:
                outs[flow["array"]][flow["rows"]] = total
    for flow in flows:
        for copy in flow["copies"]:
            copy.wait_send()


def finish_kernel(*refs):
    for source, out in zip(refs[:3], refs[3:]):
        out[...] = source[...]


def per_device(head_emb, tail_emb, relations, head_index, tail_index, rel_index, neg_index):
    heads_n, tails_n = lax.axis_size("head"), lax.axis_size("tail")
    width = relations.shape[1]
    own_rows = relations.shape[0]
    count_rel = own_rows * heads_n * tails_n // width
    heads, tails = head_emb[0], tail_emb[0]
    n_head, n_tail = heads.shape[0], tails.shape[0]
    steps, per_step, batch = head_index.shape[2:]
    negs = neg_index.shape[4]
    blocks = steps * per_step
    each = batch + negs
    lanes = (count_rel + 128) // 128 * 128
    vmem = pl.BlockSpec(memory_space=pltpu.VMEM)
    shape = jax.ShapeDtypeStruct

    bits = Bits([("head", heads_n), ("tail", tails_n)])
    count = len(bits.names)
    hb, tb = log2(heads_n), log2(tails_n)
    head_bits, tail_bits = list(range(hb)), list(range(hb, hb + tb))
    core, planar = head_bits[-1:], head_bits[:-1]
    back_planar = planar[::-1]
    gather_orders = share(own_rows, GATHER_EARLY, [
        tail_bits + planar + core, tail_bits + back_planar + core,
        planar + tail_bits + core, back_planar + tail_bits + core,
    ])
    reduce_orders = share(own_rows, REDUCE_EARLY, [
        core + planar + tail_bits[::-1], core + back_planar + tail_bits[::-1],
        core + tail_bits[::-1] + planar, core + tail_bits[::-1] + back_planar,
    ])

    indices = [
        a.reshape(blocks, 1, a.shape[-1]) for a in (head_index, tail_index, rel_index, neg_index)
    ]
    full, hv, tv, nv, offsets, head_ids, tail_ids = pl.pallas_call(
        functools.partial(gather_kernel, bits, gather_orders, tails_n, steps, count_rel),
        out_shape=(
            shape((2,) * count + (own_rows, width), F32),
            shape((blocks, batch, width), F32),
            shape((blocks, batch, width), F32),
            shape((blocks, negs, width), F32),
            shape((blocks, 1, lanes), jnp.int32),
            shape((blocks, 1, batch), jnp.int32),
            shape((1, blocks * each), jnp.int32),
        ),
        in_specs=[vmem] * 7,
        out_specs=(vmem,) * 7,
        scratch_shapes=[
            pltpu.VMEM((n_head, 2 * width), BF16),
            pltpu.VMEM((n_tail, 2 * width), BF16),
            pltpu.VMEM((2, blocks, batch, 1), jnp.int32),
            pltpu.VMEM((1, blocks, negs, 1), jnp.int32),
        ] + [pltpu.VMEM(a.shape, jnp.int32) for a in indices] + [
            pltpu.SemaphoreType.DMA((len(gather_orders) * count,)),
            pltpu.SemaphoreType.DMA((len(gather_orders) * count,)),
            pltpu.SemaphoreType.DMA((4 * steps,)),
            pltpu.SemaphoreType.DMA((4 * steps,)),
        ],
        compiler_params=pltpu.CompilerParams(
            collective_id=0, has_side_effects=True, vmem_limit_bytes=VMEM_LIMIT
        ),
        name="gather",
    )(relations, heads, tails, *indices)

    back, spread, rel_sum = pl.pallas_call(
        functools.partial(compute_kernel, count_rel),
        out_shape=(
            shape((blocks * batch, 2 * width), BF16),
            shape((blocks * each, 2 * width), BF16),
            shape((count_rel * width, width), F32),
        ),
        in_specs=[pl.BlockSpec(memory_space=pltpu.SMEM)] + [vmem] * 4,
        out_specs=(vmem,) * 3,
        scratch_shapes=[
            pltpu.VMEM((count_rel * width, width), BF16),
            pltpu.VMEM((count_rel * width, width), BF16),
            pltpu.VMEM((blocks, batch, width), F32),
            pltpu.VMEM((blocks, batch, width), F32),
            pltpu.VMEM((blocks, batch, width), F32),
        ],
        compiler_params=pltpu.CompilerParams(vmem_limit_bytes=VMEM_LIMIT),
        name="compute",
    )(offsets, full.reshape(count_rel * width, width), hv, tv, nv)

    sizes = (
        (2,) * tb + (n_head // tails_n, width),
        (2,) * hb + (n_tail // heads_n, width),
        (2,) * count + (own_rows, width),
    )
    plans = [(2, *cut) for cut in reduce_orders]
    half = sizes[1][-2] // 2
    plans += [(1, core + planar, 0, half), (1, core + back_planar, half, half)]
    plans += [(0, tail_bits[::-1], 0, sizes[0][-2])]
    buffers, sems = [], 0
    for array, order, first, rows in plans:
        for stage in range(len(order)):
            buffers.append(pltpu.VMEM((2,) * (len(order) - 1 - stage) + (rows, width), F32))
        sems += len(order)
    shares = tuple(shape(a[-2:], F32) for a in sizes)
    totals = pl.pallas_call(
        functools.partial(reduce_kernel, bits, plans),
        out_shape=shares,
        in_specs=[vmem] * 5,
        out_specs=(vmem,) * 3,
        scratch_shapes=[pltpu.VMEM(sizes[0], F32), pltpu.VMEM(sizes[1], F32)] + buffers
        + [pltpu.SemaphoreType.DMA((sems,)), pltpu.SemaphoreType.DMA((sems,))],
        compiler_params=pltpu.CompilerParams(
            collective_id=1, has_side_effects=True, vmem_limit_bytes=VMEM_LIMIT
        ),
        name="reduce",
    )(rel_sum.reshape(sizes[2]), spread, back, tail_ids, head_ids)
    head_share, tail_share, rel_share = pl.pallas_call(
        finish_kernel,
        out_shape=shares,
        in_specs=[vmem] * 3,
        out_specs=(vmem,) * 3,
        name="finish",
    )(*totals)
    return (head_share[None], tail_share[None], rel_share)


def solution(mesh):
    placed = (
        P("head", None, None),
        P("tail", None, None),
        P(("head", "tail"), None),
        P("head", "tail", None, None, None),
        P("head", "tail", None, None, None),
        P("head", "tail", None, None, None),
        P("head", "tail", None, None, None),
    )
    return jax.shard_map(
        per_device,
        mesh=mesh,
        in_specs=placed,
        out_specs=(P("head", "tail", None), P("tail", "head", None), P(("head", "tail"), None)),
        check_vma=False,
    )
```

```python
import functools
import jax
import jax.numpy as jnp
from jax import lax
from jax.experimental import pallas as pl
from jax.experimental.pallas import tpu as pltpu
from jax.sharding import PartitionSpec as P

F32 = jnp.float32
BF16 = jnp.bfloat16
VMEM_LIMIT = 60 * 1024 * 1024
GATHER_EARLY = 0.375
REDUCE_EARLY = 0.375
NN = (((1,), (0,)), ((), ()))
NT = (((1,), (1,)), ((), ()))
TN = (((0,), (0,)), ((), ()))


def split(x):
    high = x.astype(BF16)
    return high, (x - high.astype(F32)).astype(BF16)


def dot(a, b, dims):
    return lax.dot_general(a, b, dims, preferred_element_type=F32)


def dot3(a, b, dims):
    return dot(a[0], b[0], dims) + (dot(a[0], b[1], dims) + dot(a[1], b[0], dims))


def log2(n):
    assert n & (n - 1) == 0
    return n.bit_length() - 1


class Bits:
    def __init__(self, sizes):
        self.names = [(axis, bit) for axis, size in sizes for bit in reversed(range(log2(size)))]

    def mine(self, i):
        axis, bit = self.names[i]
        return lax.rem(lax.axis_index(axis) // (1 << bit), 2)

    def partner(self, i):
        axis, bit = self.names[i]
        here = lax.axis_index(axis)
        return {axis: here + (1 << bit) * (1 - 2 * self.mine(i))}


def share(rows, early, orders):
    small = max(8, int(rows * early / 16) * 8)
    big = rows // 2 - small
    cuts, first = [], 0
    for order, size in zip(orders, (big, big, small, small)):
        cuts.append((order, first, size))
        first += size
    return cuts


def meet(partners):
    barrier = pltpu.get_barrier_semaphore()
    for device in partners:
        pl.semaphore_signal(barrier, inc=1, device_id=device, device_id_type=pl.DeviceIdType.MESH)
    pl.semaphore_wait(barrier, len(partners))


def column(row):
    return jnp.transpose(jnp.broadcast_to(row, (8, row.shape[1])))[:, :1]


def gather_kernel(
    bits, orders, tails_n, steps, count_rel, *refs,
):
    rel_ref, heads_ref, tails_ref = refs[:3]
    sent_idx = refs[3:7]
    full_ref, hv_ref, tv_ref, nv_ref, off_ref, head_ids, tail_ids = refs[7:14]
    heads_cat, tails_cat, cols, neg_cols = refs[14:18]
    got_idx = refs[18:22]
    send_sem, recv_sem, idx_send, idx_recv = refs[22:]
    count = len(bits.names)
    parts = len(orders)
    mine = [bits.mine(i) for i in range(count)]
    partner = [bits.partner(i) for i in range(count)]
    blocks, batch = hv_ref.shape[:2]
    negs = nv_ref.shape[1]
    per_step = blocks // steps
    width = heads_ref.shape[1]

    me = lax.axis_index("tail")
    around, moves = [], []
    for s in range(steps):
        if s % tails_n:
            to = {"tail": lax.rem(me + tails_n - s % tails_n, tails_n)}
            around += [to, {"tail": lax.rem(me + s % tails_n, tails_n)}]
            moves.append((s, to))
    meet(partner + around)
    idx_copies = []
    for s, to in moves:
        for a in range(4):
            at = pl.ds(s * per_step, per_step)
            sem = len(idx_copies)
            copy = pltpu.make_async_remote_copy(
                src_ref=sent_idx[a].at[at],
                dst_ref=got_idx[a].at[at],
                send_sem=idx_send.at[sem],
                recv_sem=idx_recv.at[sem],
                device_id=to,
                device_id_type=pl.DeviceIdType.MESH,
            )
            copy.start()
            idx_copies.append(copy)

    def start(part, stage):
        order, first, rows = orders[part]
        done = set(order[:stage])
        where = tuple(slice(None) if i in done else mine[i] for i in range(count))
        where = where + (pl.ds(first, rows),)
        source = rel_ref.at[pl.ds(first, rows)] if stage == 0 else full_ref.at[where]
        copy = pltpu.make_async_remote_copy(
            src_ref=source,
            dst_ref=full_ref.at[where],
            send_sem=send_sem.at[part * count + stage],
            recv_sem=recv_sem.at[part * count + stage],
            device_id=partner[order[stage]],
            device_id_type=pl.DeviceIdType.MESH,
        )
        copy.start()
        return copy

    copies = [[start(part, 0)] for part in range(parts)]
    full_ref[tuple(mine)] = rel_ref[...]

    def halves(source, cat):
        high, low = split(source[...])
        cat[:, :width] = high
        cat[:, width:] = low

    def arrive():
        for copy in idx_copies:
            copy.wait_recv()

    def order_block(b):
        moved = (b // per_step) % tails_n != 0
        row = [(got_idx if moved else sent_idx)[a][b] for a in range(4)]
        rel = column(row[2])
        lanes = off_ref.shape[2]
        lane = lax.broadcasted_iota(jnp.int32, (batch, lanes), 1)
        base = jnp.sum((rel < lane).astype(jnp.int32), axis=0, keepdims=True)
        off_ref[b] = base
        same = rel == lane
        earlier = (
            lax.broadcasted_iota(jnp.int32, (batch, batch), 1)
            < lax.broadcasted_iota(jnp.int32, (batch, batch), 0)
        ).astype(BF16)
        rank = dot(earlier, same.astype(BF16), NN).astype(jnp.int32)
        place = jnp.sum(jnp.where(same, rank + base, 0), axis=1, keepdims=True)
        to = place == lax.broadcasted_iota(jnp.int32, (batch, batch), 1)
        ids = [jnp.sum(jnp.where(to, column(row[a]), 0), axis=0, keepdims=True) for a in (0, 1)]
        head_ids[b] = ids[0]
        tail_ids[:, b * (batch + negs):b * (batch + negs) + batch] = ids[1]
        tail_ids[:, b * (batch + negs) + batch:(b + 1) * (batch + negs)] = row[3]
        cols[0, b] = column(ids[0])
        cols[1, b] = column(ids[1])
        neg_cols[0, b] = column(row[3])

    def take(source, which, b, cat, out):
        tile = 128

        def body(t, carry):
            at = pl.ds(pl.multiple_of(t * tile, tile), tile)
            ids = source[which, b, at]
            hot = (ids == lax.broadcasted_iota(jnp.int32, (tile, cat.shape[0]), 1)).astype(BF16)
            both = dot(hot, cat[...], NN)
            out[b, at] = both[:, :width] + both[:, width:]
            return carry

        lax.fori_loop(0, out.shape[1] // tile, body, 0)

    work = [lambda: (halves(heads_ref, heads_cat), halves(tails_ref, tails_cat)), arrive]
    work += [functools.partial(order_block, b) for b in range(blocks)]
    work += [functools.partial(take, cols, 0, b, heads_cat, hv_ref) for b in range(blocks)]
    work += [functools.partial(take, cols, 1, b, tails_cat, tv_ref) for b in range(blocks)]
    work += [functools.partial(take, neg_cols, 0, b, tails_cat, nv_ref) for b in range(blocks)]
    done = 0
    for stage in range(count):
        upto = -(-len(work) * (stage + 1) // count)
        for job in work[done:upto]:
            job()
        done = upto
        for part in range(parts):
            copies[part][stage].wait_recv()
            if stage + 1 < count:
                copies[part].append(start(part, stage + 1))
    for copy in idx_copies:
        copy.wait_send()
    for part in range(parts):
        for copy in copies[part]:
            copy.wait_send()


def compute_kernel(
    relations, off_ref, rel_ref, hv_ref, tv_ref, nv_ref,
    back_ref, spread, grad_ref,
    rel_hi, rel_lo, query, factor, through,
):
    blocks, batch, width = hv_ref.shape
    negs = nv_ref.shape[1]
    window = 64
    row_id = lax.broadcasted_iota(jnp.int32, (window, 1), 0)

    def halve(r, carry):
        at = pl.ds(pl.multiple_of(r * width, width), width)
        rel_hi[at], rel_lo[at] = split(rel_ref[at])
        return carry

    lax.fori_loop(0, relations, halve, 0)
    query[...] = jnp.zeros_like(query)
    through[...] = jnp.zeros_like(through)

    def over_windows(step, after=None):
        def one(r, carry):
            low = [off_ref[b, 0, r] for b in range(blocks)]
            high = [off_ref[b, 0, r + 1] for b in range(blocks)]
            base = [low[b] // 8 * 8 for b in range(blocks)]
            trips = jnp.int32(0)
            for b in range(blocks):
                here = jnp.where(high[b] > low[b], (high[b] - base[b] + window - 1) // window, 0)
                trips = jnp.maximum(trips, here)
            at_r = pl.ds(pl.multiple_of(r * width, width), width)

            def inner(w, c):
                places, masks = [], []
                for b in range(blocks):
                    begin = base[b] + w * window
                    at = pl.multiple_of(jnp.minimum(begin, batch - window), 8)
                    first = jnp.maximum(low[b], begin)
                    last = jnp.minimum(high[b], begin + window)
                    ids = row_id + at
                    places.append(pl.ds(at, window))
                    masks.append(jnp.logical_and(ids >= first, ids < last))
                step(at_r, places, masks)
                return c

            lax.fori_loop(0, trips, inner, 0)
            return carry

        lax.fori_loop(0, relations, one, 0)

    def masked(ref, places, masks):
        return jnp.concatenate(
            [jnp.where(masks[b], ref[b, places[b]], 0.0) for b in range(blocks)], axis=0
        )

    def apply(source, out, dims):
        def step(at_r, places, masks):
            x = split(masked(source, places, masks))
            y = dot3(x, (rel_hi[at_r], rel_lo[at_r]), dims)
            for b in range(blocks):
                out[b, places[b]] += y[b * window:(b + 1) * window]
        return step

    over_windows(apply(hv_ref, query, NN))

    for b in range(blocks):
        q = query[b]
        tv = tv_ref[b]
        q2 = split(q)
        n2 = split(nv_ref[b])
        positive = jnp.sum(q * tv, axis=1, keepdims=True)
        coef = -jax.nn.sigmoid(-positive)
        weights = split(jax.nn.sigmoid(dot3(q2, n2, NT)) / negs)
        factor[b] = coef * tv + dot3(weights, n2, NN)
        rows = jnp.concatenate([coef * q, dot3(weights, q2, TN)], axis=0)
        high, low = split(rows)
        at = pl.ds(b * (batch + negs), batch + negs)
        spread[at, :width] = high
        spread[at, width:] = low

    grad_ref[...] = jnp.zeros_like(grad_ref)

    def outer(at_r, places, masks):
        x = split(masked(hv_ref, places, masks))
        f = split(jnp.concatenate([factor[b, places[b]] for b in range(blocks)], axis=0))
        grad_ref[at_r] += dot3(x, f, TN)

    back = apply(factor, through, NT)

    def both_ways(at_r, places, masks):
        outer(at_r, places, masks)
        back(at_r, places, masks)

    over_windows(both_ways)

    for b in range(blocks):
        high, low = split(through[b])
        back_ref[pl.ds(b * batch, batch), :width] = high
        back_ref[pl.ds(b * batch, batch), width:] = low


def reduce_kernel(bits, plans, grad_ref, spread, back, tail_ids, head_ids, *refs):
    outs = refs[:3]
    head_sum, tail_sum = refs[3:5]
    buffers = refs[5:-2]
    send_sem, recv_sem = refs[-2:]
    inputs = (head_sum, tail_sum, grad_ref)
    width = grad_ref.shape[-1]
    mine = [bits.mine(i) for i in range(len(bits.names))]
    partner = [bits.partner(i) for i in range(len(bits.names))]
    meet(partner)
    flows = []
    sem = 0
    buf = 0
    for array, order, first, rows in plans:
        flows.append(dict(
            array=array, order=order, rows=pl.ds(first, rows), sem=sem,
            buffers=buffers[buf:buf + len(order)], left=sorted(order), copies=[],
        ))
        sem += len(order)
        buf += len(order)

    def cut(flow, stage, bit, value):
        place = flow["left"].index(bit)
        where = (slice(None),) * place + (value,)
        if stage == 0:
            where = where + (slice(None),) * (len(flow["left"]) - place - 1) + (flow["rows"],)
            return inputs[flow["array"]], where
        return flow["buffers"][stage - 1], where

    def start(flow, stage):
        bit = flow["order"][stage]
        ref, where = cut(flow, stage, bit, 1 - mine[bit])
        copy = pltpu.make_async_remote_copy(
            src_ref=ref.at[where],
            dst_ref=flow["buffers"][stage],
            send_sem=send_sem.at[flow["sem"] + stage],
            recv_sem=recv_sem.at[flow["sem"] + stage],
            device_id=partner[bit],
            device_id_type=pl.DeviceIdType.MESH,
        )
        copy.start()
        flow["copies"].append(copy)

    def begin(array):
        for flow in flows:
            if flow["array"] == array:
                start(flow, 0)

    def scatter(ids, source, out):
        dims = len(out.shape) - 2
        rows = out.shape[-2]

        def body(t, carry):
            hot = (ids == lax.broadcasted_iota(jnp.int32, (rows, ids.shape[1]), 0) + t * rows)
            both = dot(hot.astype(BF16), source[...], NN)
            where = tuple(lax.rem(t // (1 << i), 2) for i in reversed(range(dims)))
            out[where] = both[:, :width] + both[:, width:]
            return carry

        lax.fori_loop(0, 1 << dims, body, 0)

    begin(2)
    heads = jnp.concatenate([head_ids[b] for b in range(head_ids.shape[0])], axis=1)
    scatter(heads, back, head_sum)
    begin(0)
    scatter(tail_ids[...], spread, tail_sum)
    begin(1)
    for stage in range(len(bits.names)):
        for flow in flows:
            order = flow["order"]
            if stage >= len(order):
                continue
            flow["copies"][stage].wait_recv()
            ref, where = cut(flow, stage, order[stage], mine[order[stage]])
            total = flow["buffers"][stage][...] + ref[where]
            flow["left"].remove(order[stage])
            if stage + 1 < len(order):
                flow["buffers"][stage][...] = total
                start(flow, stage + 1)
            else:
                outs[flow["array"]][flow["rows"]] = total
    for flow in flows:
        for copy in flow["copies"]:
            copy.wait_send()


def finish_kernel(*refs):
    for source, out in zip(refs[:3], refs[3:]):
        out[...] = source[...]


def per_device(head_emb, tail_emb, relations, head_index, tail_index, rel_index, neg_index):
    heads_n, tails_n = lax.axis_size("head"), lax.axis_size("tail")
    width = relations.shape[1]
    own_rows = relations.shape[0]
    count_rel = own_rows * heads_n * tails_n // width
    heads, tails = head_emb[0], tail_emb[0]
    n_head, n_tail = heads.shape[0], tails.shape[0]
    steps, per_step, batch = head_index.shape[2:]
    negs = neg_index.shape[4]
    blocks = steps * per_step
    each = batch + negs
    lanes = (count_rel + 128) // 128 * 128
    vmem = pl.BlockSpec(memory_space=pltpu.VMEM)
    shape = jax.ShapeDtypeStruct

    bits = Bits([("head", heads_n), ("tail", tails_n)])
    count = len(bits.names)
    hb, tb = log2(heads_n), log2(tails_n)
    head_bits, tail_bits = list(range(hb)), list(range(hb, hb + tb))
    core, planar = head_bits[-1:], head_bits[:-1]
    back_planar = planar[::-1]
    gather_orders = share(own_rows, GATHER_EARLY, [
        tail_bits + planar + core, tail_bits + back_planar + core,
        planar + tail_bits + core, back_planar + tail_bits + core,
    ])
    reduce_orders = share(own_rows, REDUCE_EARLY, [
        core + planar + tail_bits[::-1], core + back_planar + tail_bits[::-1],
        core + tail_bits[::-1] + planar, core + tail_bits[::-1] + back_planar,
    ])

    indices = [
        a.reshape(blocks, 1, a.shape[-1]) for a in (head_index, tail_index, rel_index, neg_index)
    ]
    full, hv, tv, nv, offsets, head_ids, tail_ids = pl.pallas_call(
        functools.partial(gather_kernel, bits, gather_orders, tails_n, steps, count_rel),
        out_shape=(
            shape((2,) * count + (own_rows, width), F32),
            shape((blocks, batch, width), F32),
            shape((blocks, batch, width), F32),
            shape((blocks, negs, width), F32),
            shape((blocks, 1, lanes), jnp.int32),
            shape((blocks, 1, batch), jnp.int32),
            shape((1, blocks * each), jnp.int32),
        ),
        in_specs=[vmem] * 7,
        out_specs=(vmem,) * 7,
        scratch_shapes=[
            pltpu.VMEM((n_head, 2 * width), BF16),
            pltpu.VMEM((n_tail, 2 * width), BF16),
            pltpu.VMEM((2, blocks, batch, 1), jnp.int32),
            pltpu.VMEM((1, blocks, negs, 1), jnp.int32),
        ] + [pltpu.VMEM(a.shape, jnp.int32) for a in indices] + [
            pltpu.SemaphoreType.DMA((len(gather_orders) * count,)),
            pltpu.SemaphoreType.DMA((len(gather_orders) * count,)),
            pltpu.SemaphoreType.DMA((4 * steps,)),
            pltpu.SemaphoreType.DMA((4 * steps,)),
        ],
        compiler_params=pltpu.CompilerParams(
            collective_id=0, has_side_effects=True, vmem_limit_bytes=VMEM_LIMIT
        ),
        name="gather",
    )(relations, heads, tails, *indices)

    back, spread, rel_sum = pl.pallas_call(
        functools.partial(compute_kernel, count_rel),
        out_shape=(
            shape((blocks * batch, 2 * width), BF16),
            shape((blocks * each, 2 * width), BF16),
            shape((count_rel * width, width), F32),
        ),
        in_specs=[pl.BlockSpec(memory_space=pltpu.SMEM)] + [vmem] * 4,
        out_specs=(vmem,) * 3,
        scratch_shapes=[
            pltpu.VMEM((count_rel * width, width), BF16),
            pltpu.VMEM((count_rel * width, width), BF16),
            pltpu.VMEM((blocks, batch, width), F32),
            pltpu.VMEM((blocks, batch, width), F32),
            pltpu.VMEM((blocks, batch, width), F32),
        ],
        compiler_params=pltpu.CompilerParams(vmem_limit_bytes=VMEM_LIMIT),
        name="compute",
    )(offsets, full.reshape(count_rel * width, width), hv, tv, nv)

    sizes = (
        (2,) * tb + (n_head // tails_n, width),
        (2,) * hb + (n_tail // heads_n, width),
        (2,) * count + (own_rows, width),
    )
    plans = [(2, *cut) for cut in reduce_orders]
    half = sizes[1][-2] // 2
    plans += [(1, core + planar, 0, half), (1, core + back_planar, half, half)]
    plans += [(0, tail_bits[::-1], 0, sizes[0][-2])]
    buffers, sems = [], 0
    for array, order, first, rows in plans:
        for stage in range(len(order)):
            buffers.append(pltpu.VMEM((2,) * (len(order) - 1 - stage) + (rows, width), F32))
        sems += len(order)
    shares = tuple(shape(a[-2:], F32) for a in sizes)
    totals = pl.pallas_call(
        functools.partial(reduce_kernel, bits, plans),
        out_shape=shares,
        in_specs=[vmem] * 5,
        out_specs=(vmem,) * 3,
        scratch_shapes=[pltpu.VMEM(sizes[0], F32), pltpu.VMEM(sizes[1], F32)] + buffers
        + [pltpu.SemaphoreType.DMA((sems,)), pltpu.SemaphoreType.DMA((sems,))],
        compiler_params=pltpu.CompilerParams(
            collective_id=1, has_side_effects=True, vmem_limit_bytes=VMEM_LIMIT
        ),
        name="reduce",
    )(rel_sum.reshape(sizes[2]), spread, back, tail_ids, head_ids)
    head_share, tail_share, rel_share = pl.pallas_call(
        finish_kernel,
        out_shape=shares,
        in_specs=[vmem] * 3,
        out_specs=(vmem,) * 3,
        name="finish",
    )(*totals)
    return (head_share[None], tail_share[None], rel_share)


def solution(mesh):
    placed = (
        P("head", None, None),
        P("tail", None, None),
        P(("head", "tail"), None),
        P("head", "tail", None, None, None),
        P("head", "tail", None, None, None),
        P("head", "tail", None, None, None),
        P("head", "tail", None, None, None),
    )
    return jax.shard_map(
        per_device,
        mesh=mesh,
        in_specs=placed,
        out_specs=(P("head", "tail", None), P("tail", "head", None), P(("head", "tail"), None)),
        check_vma=False,
    )
```
